32 devices in a mesh: gx: 8 (over z, x), gy: 4 (over y, core).
Axes of the slice: x: 2, y: 2, z: 4, core: 2. Of those that a mesh axis runs over, the one named last changes fastest.
Arguments:
- e_field: float32 [3, 128, 128, 256], P(None, 'gx', 'gy'), may hold values from -6 to 6
- h_field: float32 [3, 128, 128, 256], P(None, 'gx', 'gy'), may hold values from -6 to 6
- material: int32 [128, 128, 256], P('gx', 'gy'), may hold values from 0 to 7
- eps_table: float32 [8], replicated, may hold values from 1 to 12
- forward_dft: bfloat16 [4, 2, 3, 128, 128, 256], P(None, None, None, 'gx', 'gy'), may hold values from -6 to 6
- phase_step: float32 [4], replicated, may hold values from 0.3 to 2.8
- interp_kernels: float32 [4, 1024, 128], replicated, may hold values from -0.1875 to 0.1875
- kernel_id: int32 [64, 64], P('gx', 'gy'), may hold values from 0 to 3
- owner_map: int32 [64, 64], P('gx', 'gy'), may hold values from 0 to 31, as said below
- slot_map: int32 [64, 64], P('gx', 'gy'), may hold values from 0 to 63
Outputs:
- e_out: float32 [3, 128, 128, 256], P(None, 'gx', 'gy')
- h_out: float32 [3, 128, 128, 256], P(None, 'gx', 'gy')
- design_grad: float32 [2048, 128], P(('gx', 'gy'))
The draws below stay inside these ranges and needn't reach their ends.
Inputs may be any that keep to these rules, and one draw needn't show every extreme that they name: `owner_map`: the tiles of one device name no owner more than 8 times; in every draw one owner is named exactly 8 times by the tiles of every device.
All inputs are finite; a program needn't handle non-finite values.
Results may differ from the reference program's by a relative error of at most 0.0003.
Values sent between devices are 32-bit elements; how exact they have to be, the bound alone decides.
A program may use at most 64 MiB of HBM per device.

```python
import math
import jax
import jax.numpy as jnp
from jax import lax

CX = 16
CY = 32
NZ = 256
STEPS = 4
WAVES = 4
MATS = 8
KERNELS = 4
VOX = 128
SLOTS = 64
NX = 128
NY = 128
OWNERS = 32
TILES_DEV = 128
TILE_CELLS = 1024
CAP = 8


def draw_owner_map(key, part):
    grid_x = NX // CX
    grid_y = NY // CY
    common = jax.random.randint(jax.random.fold_in(key, 11), (), 0, OWNERS).astype(jnp.int32)

    def one_device(device):
        subkey = jax.random.fold_in(key, 1000 + device)
        order = jax.random.permutation(jax.random.fold_in(subkey, 1), TILES_DEV)
        pool = jax.random.permutation(jax.random.fold_in(subkey, 2), (OWNERS - 1) * CAP)[:TILES_DEV - CAP] // CAP
        others = (common + 1 + pool.astype(jnp.int32)) % OWNERS
        assign = jnp.concatenate([jnp.zeros((CAP,), jnp.int32) + common, others.astype(jnp.int32)])
        return jnp.zeros((TILES_DEV,), jnp.int32).at[order].set(assign)
    table = jax.vmap(one_device)(jnp.arange(OWNERS, dtype=jnp.int32))
    table = table.reshape(grid_x, grid_y, CX // 2, CY // 2).transpose(0, 2, 1, 3)
    return table.reshape(NX // 2, NY // 2)


def with_ends(array, key, low, top_value):
    longest = array.shape.index(max(array.shape))
    spots = []
    for shift in (0, 1):
        where = [jax.random.randint(jax.random.fold_in(key, axis), (), 0, length) for axis, length in enumerate(array.shape)]
        where[longest] = (where[longest] + shift) % array.shape[longest]
        spots.append(tuple(where))
    return array.at[spots[0]].set(low).at[spots[1]].set(top_value)


def block_levels(rng, shape, cuts, low, largest):
    def one(dim, parts):
        heights = jax.random.uniform(jax.random.fold_in(jax.random.fold_in(rng, 6), dim), (parts,), jnp.float32, low / len(cuts), largest / len(cuts))
        return jnp.repeat(jnp.exp(heights), shape[dim] // parts).reshape((-1,) + (1,) * (len(shape) - dim - 1))

    loudness = one(*cuts[0])
    for cut in cuts[1:]:
        loudness = loudness * one(*cut)
    return loudness


def normal_values(rng, extent, width, bound, split=(), kind=jnp.bfloat16):
    values = jax.random.normal(rng, extent, jnp.float32) * width
    if len(split) > 0:
        values = block_levels(rng, extent, split, -0.22, 0.18) * values
    return jnp.clip(values, min=-bound, max=bound).astype(kind)


def setup_inputs(seed: int = 0) -> dict:
    arg_keys = jax.random.split(jax.random.key(seed), 11)
    e_field = normal_values(arg_keys[0], (3, NX, NY, NZ), 1.0, 6.0, ((1, 8), (2, 4)), jnp.float32)
    h_field = normal_values(arg_keys[1], (3, NX, NY, NZ), 1.0, 6.0, ((1, 8), (2, 4)), jnp.float32)
    material = with_ends(jax.random.randint(arg_keys[2], (NX, NY, NZ), 0, MATS), jax.random.fold_in(arg_keys[2], 1), 0, MATS - 1).astype(jnp.int32)
    eps_table = jnp.clip(jnp.exp(jax.random.uniform(arg_keys[3], (MATS,), jnp.float32, math.log(1.0), math.log(12.0))), 1.0, 12.0)
    forward_dft = normal_values(arg_keys[4], (WAVES, 2, 3, NX, NY, NZ), 1.0, 6.0, ((3, 8), (4, 4)))
    phase_step = jnp.clip(jax.random.uniform(arg_keys[5], (WAVES,), jnp.float32, 0.3, 2.8), 0.3, 2.8)
    interp_kernels = normal_values(arg_keys[6], (KERNELS, TILE_CELLS, VOX), TILE_CELLS ** -0.5, 0.1875, (), jnp.float32)
    kernel_id = with_ends(jax.random.randint(arg_keys[7], (NX // 2, NY // 2), 0, KERNELS), jax.random.fold_in(arg_keys[7], 1), 0, KERNELS - 1).astype(jnp.int32)
    owner_map = draw_owner_map(jax.random.fold_in(arg_keys[10], 71), 0)
    slot_map = with_ends(jax.random.randint(arg_keys[9], (NX // 2, NY // 2), 0, SLOTS), jax.random.fold_in(arg_keys[9], 1), 0, SLOTS - 1).astype(jnp.int32)
    return dict(e_field=e_field, h_field=h_field, material=material, eps_table=eps_table, forward_dft=forward_dft, phase_step=phase_step, interp_kernels=interp_kernels, kernel_id=kernel_id, owner_map=owner_map, slot_map=slot_map)


COURANT = 0.5


def ahead_diff(field, axis):
    widths = [(0, 0), (0, 0), (0, 0)]
    widths[axis] = (0, 1)
    padded = jnp.pad(field, widths)
    return lax.slice_in_dim(padded, 1, field.shape[axis] + 1, axis=axis) - field


def behind_diff(field, axis):
    widths = [(0, 0), (0, 0), (0, 0)]
    widths[axis] = (1, 0)
    padded = jnp.pad(field, widths)
    return field - lax.slice_in_dim(padded, 0, field.shape[axis], axis=axis)


def reference(e_field, h_field, material, eps_table, forward_dft, phase_step, interp_kernels, kernel_id, owner_map, slot_map):
    scale = COURANT / eps_table[material]
    elec_x, elec_y, elec_z = e_field[0], e_field[1], e_field[2]
    magn_x, magn_y, magn_z = h_field[0], h_field[1], h_field[2]
    sens = jnp.zeros(elec_x.shape, jnp.float32)
    for step_index in range(STEPS):
        magn_x = magn_x - COURANT * (ahead_diff(elec_z, 1) - ahead_diff(elec_y, 2))
        magn_y = magn_y - COURANT * (ahead_diff(elec_x, 2) - ahead_diff(elec_z, 0))
        magn_z = magn_z - COURANT * (ahead_diff(elec_y, 0) - ahead_diff(elec_x, 1))
        elec_x = elec_x + scale * (behind_diff(magn_z, 1) - behind_diff(magn_y, 2))
        elec_y = elec_y + scale * (behind_diff(magn_x, 2) - behind_diff(magn_z, 0))
        elec_z = elec_z + scale * (behind_diff(magn_y, 0) - behind_diff(magn_x, 1))
        moment = float(step_index + 1)
        cosines = jnp.cos(phase_step * moment)
        sine_terms = jnp.sin(phase_step * moment)
        elec = (elec_x, elec_y, elec_z)
        for comp in range(3):
            weight = jnp.zeros(elec_x.shape, jnp.float32)
            for wave in range(WAVES):
                weight = weight + forward_dft[wave, 0, comp].astype(jnp.float32) * cosines[wave] - forward_dft[wave, 1, comp].astype(jnp.float32) * sine_terms[wave]
            sens = sens + elec[comp] * weight
    sens = sens / float(WAVES * STEPS)
    tile_rows = sens.reshape(NX // 2, 2, NY // 2, 2, NZ).transpose(0, 2, 1, 3, 4).reshape(-1, 4 * NZ)
    all_kernels = jnp.einsum('tc,kcv->tkv', tile_rows, interp_kernels, precision=lax.Precision.HIGHEST)
    selector = (kernel_id.reshape(-1)[:, None] == jnp.arange(KERNELS, dtype=jnp.int32)[None, :]).astype(jnp.float32)
    restricted = jnp.sum(all_kernels * selector[:, :, None], axis=1)
    target = owner_map.reshape(-1) * SLOTS + slot_map.reshape(-1)
    design_grad = jax.ops.segment_sum(restricted, target, num_segments=OWNERS * SLOTS)
    e_out = jnp.stack([elec_x, elec_y, elec_z])
    h_out = jnp.stack([magn_x, magn_y, magn_z])
    return (e_out, h_out, design_grad)
```

```python
import functools

import jax
import jax.numpy as jnp
from jax import lax
from jax.experimental import pallas as pl
from jax.experimental.pallas import tpu as pltpu
from jax.sharding import PartitionSpec as P

STEPS = 4
SLOTS = 64
COURANT = 0.5

F32 = jnp.float32
BF16 = jnp.bfloat16
MESH = pl.DeviceIdType.MESH


def split2(value):
    high = value.astype(BF16)
    return high, (value - high.astype(F32)).astype(BF16)


def dot(lhs, rhs):
    return jnp.dot(lhs, rhs, preferred_element_type=F32)


def dot_rows(lhs, rhs):
    return lax.dot_general(lhs, rhs, (((0,), (0,)), ((), ())), preferred_element_type=F32)


def iota(shape, dim):
    return lax.broadcasted_iota(jnp.int32, shape, dim)


def kernel(
    size_x,
    size_y,
    capacity,
    eps_ref,
    phase_ref,
    e_in,
    h_in,
    mat_in,
    dft_in,
    kern_in,
    kid_in,
    owner_in,
    slot_in,
    e_out,
    h_out,
    grad_ref,
    elec,
    magn,
    mat,
    scale,
    dft,
    kern,
    kern_high,
    kern_low,
    kid,
    owner,
    slot,
    weights,
    sens,
    halo_x,
    halo_y,
    pack_y,
    put,
    got,
    put_slot,
    got_slot,
    in_sem,
    out_sem,
    send_x,
    recv_x,
    send_y,
    recv_y,
    a2a_sem,
):
    count = size_x * size_y
    cells_x, cells_y, depth = mat.shape
    waves = dft.shape[0]
    tile_x, tile_y = kid.shape
    tiles = tile_x * tile_y
    kernels, tile_cells, voxels = kern.shape
    gx = lax.axis_index("gx")
    gy = lax.axis_index("gy")
    me = gx * size_y + gy

    loads = [
        pltpu.make_async_copy(source, target, in_sem.at[place])
        for place, (source, target) in enumerate(
            [
                (e_in, elec),
                (h_in, magn),
                (mat_in, mat),
                (kid_in, kid),
                (owner_in, owner),
                (slot_in, slot),
                (kern_in, kern),
                (dft_in, dft),
            ]
        )
    ]
    for load in loads:
        load.start()

    barrier = pltpu.get_barrier_semaphore()

    def greet(step, carry):
        peer = lax.rem(me + step, count)
        pl.semaphore_signal(
            barrier,
            inc=1,
            device_id=(peer // size_y, lax.rem(peer, size_y)),
            device_id_type=MESH,
        )
        return carry

    lax.fori_loop(1, count, greet, 0)

    row_y = iota((cells_y, depth), 0)
    col_z = iota((cells_y, depth), 1)

    def y_up(v):
        return jnp.where(row_y == cells_y - 1, 0.0, pltpu.roll(v, cells_y - 1, 0))

    def z_up(v):
        return jnp.where(col_z == depth - 1, 0.0, pltpu.roll(v, depth - 1, 1))

    def y_down(v):
        return jnp.where(row_y == 0, 0.0, pltpu.roll(v, 1, 0))

    def z_down(v):
        return jnp.where(col_z == 0, 0.0, pltpu.roll(v, 1, 1))

    def h_plane(x, last):
        ex, ey, ez = elec[0, x], elec[1, x], elec[2, x]
        dx_ey = -ey if last else elec[1, x + 1] - ey
        dx_ez = -ez if last else elec[2, x + 1] - ez
        magn[0, x] = magn[0, x] - COURANT * ((y_up(ez) - ez) - (z_up(ey) - ey))
        magn[1, x] = magn[1, x] - COURANT * ((z_up(ex) - ex) - dx_ez)
        magn[2, x] = magn[2, x] - COURANT * (dx_ey - (y_up(ex) - ex))

    def e_plane(x, first):
        hx, hy, hz = magn[0, x], magn[1, x], magn[2, x]
        dx_hy = hy if first else hy - magn[1, x - 1]
        dx_hz = hz if first else hz - magn[2, x - 1]
        factor = scale[x]
        elec[0, x] = elec[0, x] + factor * ((hz - y_down(hz)) - (hy - z_down(hy)))
        elec[1, x] = elec[1, x] + factor * ((hx - z_down(hx)) - dx_hz)
        elec[2, x] = elec[2, x] + factor * (dx_hy - (hx - y_down(hx)))

    def loop(low, high, body):
        def run(x, carry):
            body(x)
            return carry

        lax.fori_loop(low, high, run, 0)

    def h_interior():
        loop(0, cells_x - 1, lambda x: h_plane(x, False))
        h_plane(cells_x - 1, True)

    def e_interior():
        e_plane(0, True)
        loop(1, cells_x, lambda x: e_plane(x, False))

    def x_copy(half, source, shift):
        return pltpu.make_async_remote_copy(
            src_ref=source,
            dst_ref=halo_x.at[half],
            send_sem=send_x.at[half],
            recv_sem=recv_x.at[half],
            device_id=(gx + shift, gy),
            device_id_type=MESH,
        )

    def y_copy(half, shift):
        return pltpu.make_async_remote_copy(
            src_ref=pack_y.at[half],
            dst_ref=halo_y.at[half],
            send_sem=send_y.at[half],
            recv_sem=recv_y.at[half],
            device_id=(gx, gy + shift),
            device_id_type=MESH,
        )

    has_before_x, has_after_x = gx > 0, gx < size_x - 1
    has_before_y, has_after_y = gy > 0, gy < size_y - 1

    def copies(half):
        if half % 2 == 0:
            return (
                (has_before_x, has_after_x, x_copy(half, elec.at[pl.ds(1, 2), 0], -1)),
                (has_before_y, has_after_y, y_copy(half, -1)),
            )
        return (
            (has_after_x, has_before_x, x_copy(half, magn.at[pl.ds(1, 2), cells_x - 1], 1)),
            (has_after_y, has_before_y, y_copy(half, 1)),
        )

    def send(half):
        (to_x, _, over_x), (to_y, _, over_y) = copies(half)

        @pl.when(to_x)
        def _():
            over_x.start()

        field, row = (elec, 0) if half % 2 == 0 else (magn, cells_y - 1)
        pack_y[half, 0] = field[0, :, pl.ds(row, 1), :]
        pack_y[half, 1] = field[2, :, pl.ds(row, 1), :]

        @pl.when(to_y)
        def _():
            over_y.start()

    def receive(half):
        (to_x, from_x, over_x), (to_y, from_y, over_y) = copies(half)

        @pl.when(from_y)
        def _():
            over_y.wait_recv()
            if half % 2 == 0:
                row = pl.ds(cells_y - 1, 1)
                magn[0, :, row, :] = magn[0, :, row, :] - COURANT * halo_y[half, 1]
                magn[2, :, row, :] = magn[2, :, row, :] + COURANT * halo_y[half, 0]
            else:
                row = pl.ds(0, 1)
                factor = scale[:, row, :]
                elec[0, :, row, :] = elec[0, :, row, :] - factor * halo_y[half, 1]
                elec[2, :, row, :] = elec[2, :, row, :] + factor * halo_y[half, 0]

        @pl.when(from_x)
        def _():
            over_x.wait_recv()
            if half % 2 == 0:
                last = cells_x - 1
                magn[1, last] = magn[1, last] + COURANT * halo_x[half, 1]
                magn[2, last] = magn[2, last] - COURANT * halo_x[half, 0]
            else:
                factor = scale[0]
                elec[1, 0] = elec[1, 0] + factor * halo_x[half, 1]
                elec[2, 0] = elec[2, 0] - factor * halo_x[half, 0]

        @pl.when(to_x)
        def _():
            over_x.wait_send()

        @pl.when(to_y)
        def _():
            over_y.wait_send()

    def make_scale():
        def plane(x):
            kind = mat[x]
            eps = jnp.full(kind.shape, eps_ref[0], F32)
            for index in range(1, eps_ref.shape[0]):
                eps = jnp.where(kind == index, eps_ref[index], eps)
            scale[x] = COURANT / eps

        loop(0, cells_x, plane)

    def make_coefs():
        width = 2 * waves * cells_y
        column = iota((8, width), 1)
        wave = column // (2 * cells_y)
        phase = jnp.full((8, width), phase_ref[0], F32)
        for index in range(1, waves):
            phase = jnp.where(wave == index, phase_ref[index], phase)
        angle = phase * (iota((8, width), 0) + 1).astype(F32)
        imaginary = lax.rem(column // cells_y, 2) == 1
        values = jnp.where(imaginary, -jnp.sin(angle), jnp.cos(angle)) / float(waves * STEPS)
        own = iota((cells_y, width), 0) == lax.rem(iota((cells_y, width), 1), cells_y)
        table = jnp.concatenate(
            [jnp.where(own, values[step : step + 1], 0.0) for step in range(STEPS)], axis=0
        )
        return jnp.concatenate(split2(table), axis=0)

    def make_weights(low, high):
        coefs = make_coefs()
        half = STEPS * cells_y

        def plane(index):
            comp, x = index // cells_x, lax.rem(index, cells_x)
            block = dft[:, :, comp, x].reshape(2 * waves * cells_y, depth)
            both = dot(coefs, block)
            weights[:, comp, x] = (both[:half] + both[half:]).reshape(STEPS, cells_y, depth)

        loop(low * cells_x, high * cells_x, plane)

    def add_sens(step):
        def plane(x):
            total = elec[0, x] * weights[step, 0, x]
            total = total + elec[1, x] * weights[step, 1, x]
            total = total + elec[2, x] * weights[step, 2, x]
            for block in range(depth // 128):
                lanes = total[:, block * 128 : (block + 1) * 128]
                sens[block, x] = lanes if step == 0 else sens[block, x] + lanes

        loop(0, cells_x, plane)

    def as_column(values):
        pick = (iota((tiles, tile_x), 0) // tile_y == iota((tiles, tile_x), 1)).astype(BF16)
        spread = dot(pick, values.astype(F32).astype(BF16))
        keep = iota((tiles, tile_y), 1) == lax.rem(iota((tiles, tile_y), 0), tile_y)
        return jnp.sum(jnp.where(keep, spread, 0.0), axis=1, keepdims=True)

    def as_row(values):
        rows, lanes = values.shape
        size = rows * lanes
        pick = (iota((rows, size), 1) // lanes == iota((rows, size), 0)).astype(BF16)
        spread = dot_rows(values.astype(F32).astype(BF16), pick)
        keep = iota((lanes, size), 0) == lax.rem(iota((lanes, size), 1), lanes)
        return jnp.sum(jnp.where(keep, spread, 0.0), axis=0, keepdims=True)

    def positions():
        own_row = as_row(owner[...])
        own_column = as_column(owner[...])
        earlier = (own_column == own_row) & (iota((tiles, tiles), 0) < iota((tiles, tiles), 1))
        rank = jnp.sum(jnp.where(earlier, 1.0, 0.0), axis=0, keepdims=True)
        return own_row, own_column, rank

    def send_slots():
        own_row, _, rank = positions()
        mine = (iota((count, tiles), 0).astype(F32) == own_row).astype(BF16)
        place = (iota((128, tiles), 0).astype(F32) == rank).astype(F32)
        labels = (place * (as_row(slot[...]) + 1.0)).astype(BF16)
        table = (
            lax.dot_general(mine, labels, (((1,), (1,)), ((), ())), preferred_element_type=F32)
            - 1.0
        )
        put_slot[...] = table.reshape(count, 1, 128)
        got_slot[me] = put_slot[me]

        def push(step, carry):
            peer = lax.rem(me + step, count)
            pltpu.make_async_remote_copy(
                src_ref=put_slot.at[peer],
                dst_ref=got_slot.at[me],
                send_sem=a2a_sem.at[0],
                recv_sem=a2a_sem.at[1],
                device_id=(peer // size_y, lax.rem(peer, size_y)),
                device_id_type=MESH,
            ).start()
            return carry

        lax.fori_loop(1, count, push, 0)

    def wait_all(buffer, place):
        part = buffer.at[pl.ds(0, count - 1)]
        pltpu.make_async_copy(part, part, a2a_sem.at[place]).wait()

    def make_kernels():
        for index in range(kernels):
            high, low = split2(kern[index])
            kern_high[:, index * voxels : (index + 1) * voxels] = high
            kern_low[:, index * voxels : (index + 1) * voxels] = low

    loads[0].wait()
    pl.semaphore_wait(barrier, count - 1)
    send(0)
    loads[1].wait()
    h_interior()
    loads[2].wait()
    make_scale()
    receive(0)
    send(1)
    e_interior()
    loads[7].wait()
    make_weights(0, 2)
    receive(1)
    send(2)
    h_interior()
    make_weights(2, 3)
    add_sens(0)
    receive(2)
    send(3)
    e_interior()
    for place in (3, 4, 5):
        loads[place].wait()
    send_slots()
    receive(3)
    send(4)
    h_interior()
    add_sens(1)
    receive(4)
    send(5)
    e_interior()
    loads[6].wait()
    make_kernels()
    receive(5)
    send(6)
    h_interior()
    add_sens(2)
    receive(6)
    send(7)
    store_h = pltpu.make_async_copy(magn, h_out, out_sem.at[0])
    store_h.start()
    e_interior()
    wait_all(put_slot, 0)
    wait_all(got_slot, 1)
    receive(7)
    store_e = pltpu.make_async_copy(elec, e_out, out_sem.at[1])
    store_e.start()
    add_sens(3)

    total = jnp.zeros((tiles, kernels * voxels), F32)
    for a in range(2):
        for b in range(2):
            part = [
                sens[block, pl.ds(a, cells_x // 2, 2), pl.ds(b, cells_y // 2, 2), :]
                for block in range(depth // 128)
            ]
            part = jnp.concatenate([lanes.reshape(tiles, 128) for lanes in part], axis=1)
            high, low = split2(part)
            rows = slice((2 * a + b) * depth, (2 * a + b + 1) * depth)
            big, small = kern_high[rows, :], kern_low[rows, :]
            total = total + dot(high, big) + (dot(low, big) + dot(high, small))
    kinds = as_column(kid[...])
    restricted = jnp.zeros((tiles, voxels), F32)
    for index in range(kernels):
        restricted = restricted + jnp.where(
            kinds == float(index), total[:, index * voxels : (index + 1) * voxels], 0.0
        )

    own_row, _, rank = positions()
    position = own_row * float(capacity) + rank
    placement = (iota((count * capacity, tiles), 0).astype(F32) == position).astype(BF16)
    high, low = split2(restricted)
    put[...] = (dot(placement, high) + dot(placement, low)).reshape(count, capacity, voxels)
    got[me] = put[me]

    def push(step, carry):
        peer = lax.rem(me + step, count)
        pltpu.make_async_remote_copy(
            src_ref=put.at[peer],
            dst_ref=got.at[me],
            send_sem=a2a_sem.at[2],
            recv_sem=a2a_sem.at[3],
            device_id=(peer // size_y, lax.rem(peer, size_y)),
            device_id_type=MESH,
        ).start()
        return carry

    lax.fori_loop(1, count, push, 0)
    received = got_slot[...].reshape(count, 128)[:, :capacity]
    gather = (
        iota((SLOTS, count * capacity), 0).astype(F32) == as_row(received)
    ).astype(BF16)
    wait_all(got, 3)
    high, low = split2(got[...].reshape(count * capacity, voxels))
    grad_ref[...] = dot(gather, high) + dot(gather, low)
    wait_all(put, 2)
    store_h.wait()
    store_e.wait()


def per_device(
    size_x,
    size_y,
    e_field,
    h_field,
    material,
    eps_table,
    forward_dft,
    phase_step,
    interp_kernels,
    kernel_id,
    owner_map,
    slot_map,
):
    count = size_x * size_y
    cells_x, cells_y, depth = material.shape
    kernels, tile_cells, voxels = interp_kernels.shape
    tiles = cells_x * cells_y // 4
    capacity = max(2, (2 * tiles + count - 1) // count)
    field = jax.ShapeDtypeStruct(e_field.shape, F32)
    anywhere = pl.BlockSpec(memory_space=pl.ANY)
    halves = 2 * STEPS
    return pl.pallas_call(
        functools.partial(kernel, size_x, size_y, capacity),
        out_shape=(field, field, jax.ShapeDtypeStruct((SLOTS, voxels), F32)),
        in_specs=[pl.BlockSpec(memory_space=pltpu.SMEM)] * 2 + [anywhere] * 8,
        out_specs=(anywhere, anywhere, pl.BlockSpec(memory_space=pltpu.VMEM)),
        scratch_shapes=[
            pltpu.VMEM(e_field.shape, F32),
            pltpu.VMEM(h_field.shape, F32),
            pltpu.VMEM(material.shape, jnp.int32),
            pltpu.VMEM(material.shape, F32),
            pltpu.VMEM(forward_dft.shape, BF16),
            pltpu.VMEM(interp_kernels.shape, F32),
            pltpu.VMEM((tile_cells, kernels * voxels), BF16),
            pltpu.VMEM((tile_cells, kernels * voxels), BF16),
            pltpu.VMEM(kernel_id.shape, jnp.int32),
            pltpu.VMEM(owner_map.shape, jnp.int32),
            pltpu.VMEM(slot_map.shape, jnp.int32),
            pltpu.VMEM((STEPS,) + e_field.shape, F32),
            pltpu.VMEM((depth // 128, cells_x, cells_y, 128), F32),
            pltpu.VMEM((halves, 2, cells_y, depth), F32),
            pltpu.VMEM((halves, 2, cells_x, 1, depth), F32),
            pltpu.VMEM((halves, 2, cells_x, 1, depth), F32),
            pltpu.VMEM((count, capacity, voxels), F32),
            pltpu.VMEM((count, capacity, voxels), F32),
            pltpu.VMEM((count, 1, 128), F32),
            pltpu.VMEM((count, 1, 128), F32),
            pltpu.SemaphoreType.DMA((8,)),
            pltpu.SemaphoreType.DMA((2,)),
            pltpu.SemaphoreType.DMA((halves,)),
            pltpu.SemaphoreType.DMA((halves,)),
            pltpu.SemaphoreType.DMA((halves,)),
            pltpu.SemaphoreType.DMA((halves,)),
            pltpu.SemaphoreType.DMA((4,)),
        ],
        compiler_params=pltpu.CompilerParams(
            collective_id=0, has_side_effects=True, vmem_limit_bytes=60 * 2**20
        ),
    )(
        eps_table,
        phase_step,
        e_field,
        h_field,
        material,
        forward_dft,
        interp_kernels,
        kernel_id,
        owner_map,
        slot_map,
    )


def solution(mesh):
    return jax.shard_map(
        functools.partial(per_device, mesh.shape["gx"], mesh.shape["gy"]),
        mesh=mesh,
        in_specs=(
            P(None, "gx", "gy", None),
            P(None, "gx", "gy", None),
            P("gx", "gy", None),
            P(),
            P(None, None, None, "gx", "gy", None),
            P(),
            P(),
            P("gx", "gy"),
            P("gx", "gy"),
            P("gx", "gy"),
        ),
        out_specs=(P(None, "gx", "gy", None), P(None, "gx", "gy", None), P(("gx", "gy"), None)),
        check_vma=False,
    )
```

```python
import functools

import jax
import jax.numpy as jnp
from jax import lax
from jax.experimental import pallas as pl
from jax.experimental.pallas import tpu as pltpu
from jax.sharding import PartitionSpec as P

STEPS = 4
SLOTS = 64
COURANT = 0.5
UNROLL = 4

F32 = jnp.float32
BF16 = jnp.bfloat16
MESH = pl.DeviceIdType.MESH


def split2(value):
    high = value.astype(BF16)
    return high, (value - high.astype(F32)).astype(BF16)


def dot(lhs, rhs):
    return jnp.dot(lhs, rhs, preferred_element_type=F32)


def dot_rows(lhs, rhs):
    return lax.dot_general(lhs, rhs, (((0,), (0,)), ((), ())), preferred_element_type=F32)


def iota(shape, dim):
    return lax.broadcasted_iota(jnp.int32, shape, dim)


def as_row(values):
    rows, lanes = values.shape
    size = rows * lanes
    pick = (iota((rows, size), 1) // lanes == iota((rows, size), 0)).astype(BF16)
    spread = dot_rows(values.astype(F32).astype(BF16), pick)
    keep = iota((lanes, size), 0) == lax.rem(iota((lanes, size), 1), lanes)
    return jnp.sum(jnp.where(keep, spread, 0.0), axis=0, keepdims=True)


def kernel(
    size_x,
    size_y,
    capacity,
    eps_ref,
    phase_ref,
    e_in,
    h_in,
    mat_in,
    dft_in,
    kern_in,
    kid_in,
    owner_in,
    slot_in,
    last_elec,
    magn,
    put_out,
    slot_out,
    elec_steps,
    mat,
    scale,
    dft,
    kern,
    kern_high,
    kern_low,
    kid,
    owner,
    slot,
    coefs,
    weights,
    sens,
    halo_x,
    halo_y,
    pack_y,
    put,
    put_slot,
    in_sem,
    send_x,
    recv_x,
    send_y,
    recv_y,
    a2a_sem,
):
    count = size_x * size_y
    cells_x, cells_y, depth = mat.shape
    waves = dft.shape[0]
    tile_x, tile_y = kid.shape
    tiles = tile_x * tile_y
    kernels, tile_cells, voxels = kern.shape
    gx = lax.axis_index("gx")
    gy = lax.axis_index("gy")
    me = gx * size_y + gy

    got, got_slot = put_out, slot_out
    elec = [elec_steps.at[step] for step in range(STEPS)] + [last_elec]

    loads = [
        pltpu.make_async_copy(source, target, in_sem.at[place])
        for place, (source, target) in enumerate(
            [
                (e_in, elec[0]),
                (h_in, magn),
                (mat_in, mat),
                (kid_in, kid),
                (owner_in, owner),
                (slot_in, slot),
                (kern_in, kern),
                (dft_in, dft),
            ]
        )
    ]
    for load in loads:
        load.start()

    barrier = pltpu.get_barrier_semaphore()

    def greet(step, carry):
        peer = lax.rem(me + step, count)
        pl.semaphore_signal(
            barrier,
            inc=1,
            device_id=(peer // size_y, lax.rem(peer, size_y)),
            device_id_type=MESH,
        )
        return carry

    lax.fori_loop(1, count, greet, 0)

    row_y = iota((cells_y, depth), 0)
    col_z = iota((cells_y, depth), 1)

    def y_up(v):
        return jnp.where(row_y == cells_y - 1, 0.0, pltpu.roll(v, cells_y - 1, 0))

    def z_up(v):
        return jnp.where(col_z == depth - 1, 0.0, pltpu.roll(v, depth - 1, 1))

    def y_down(v):
        return jnp.where(row_y == 0, 0.0, pltpu.roll(v, 1, 0))

    def z_down(v):
        return jnp.where(col_z == 0, 0.0, pltpu.roll(v, 1, 1))

    def h_plane(step, x, last):
        elec_now = elec[step]
        ex, ey, ez = elec_now[0, x], elec_now[1, x], elec_now[2, x]
        dx_ey = -ey if last else elec_now[1, x + 1] - ey
        dx_ez = -ez if last else elec_now[2, x + 1] - ez
        magn[0, x] = magn[0, x] - COURANT * ((y_up(ez) - ez) - (z_up(ey) - ey))
        magn[1, x] = magn[1, x] - COURANT * ((z_up(ex) - ex) - dx_ez)
        magn[2, x] = magn[2, x] - COURANT * (dx_ey - (y_up(ex) - ex))

    def e_plane(step, x, first):
        elec_now, elec_new = elec[step], elec[step + 1]
        hx, hy, hz = magn[0, x], magn[1, x], magn[2, x]
        dx_hy = hy if first else hy - magn[1, x - 1]
        dx_hz = hz if first else hz - magn[2, x - 1]
        factor = scale[x]
        elec_new[0, x] = elec_now[0, x] + factor * ((hz - y_down(hz)) - (hy - z_down(hy)))
        elec_new[1, x] = elec_now[1, x] + factor * ((hx - z_down(hx)) - dx_hz)
        elec_new[2, x] = elec_now[2, x] + factor * (dx_hy - (hx - y_down(hx)))

    def loop(low, high, body):
        def run(x, carry):
            body(x)
            return carry

        lax.fori_loop(low, high, run, 0)

    def h_interior(step):
        loop(0, cells_x - 1, lambda x: h_plane(step, x, False))
        h_plane(step, cells_x - 1, True)

    def e_interior(step):
        e_plane(step, 0, True)
        loop(1, cells_x, lambda x: e_plane(step, x, False))

    def x_copy(half, source, shift):
        return pltpu.make_async_remote_copy(
            src_ref=source,
            dst_ref=halo_x.at[half],
            send_sem=send_x.at[half],
            recv_sem=recv_x.at[half],
            device_id=(gx + shift, gy),
            device_id_type=MESH,
        )

    def y_copy(half, shift):
        return pltpu.make_async_remote_copy(
            src_ref=pack_y.at[half],
            dst_ref=halo_y.at[half],
            send_sem=send_y.at[half],
            recv_sem=recv_y.at[half],
            device_id=(gx, gy + shift),
            device_id_type=MESH,
        )

    has_before_x, has_after_x = gx > 0, gx < size_x - 1
    has_before_y, has_after_y = gy > 0, gy < size_y - 1

    def copies(half):
        if half % 2 == 0:
            return (
                (has_before_x, has_after_x, x_copy(half, elec[half // 2].at[pl.ds(1, 2), 0], -1)),
                (has_before_y, has_after_y, y_copy(half, -1)),
            )
        return (
            (has_after_x, has_before_x, x_copy(half, magn.at[pl.ds(1, 2), cells_x - 1], 1)),
            (has_after_y, has_before_y, y_copy(half, 1)),
        )

    def send(half):
        (to_x, _, over_x), (to_y, _, over_y) = copies(half)

        @pl.when(to_x)
        def _():
            over_x.start()

        field, row = (elec[half // 2], 0) if half % 2 == 0 else (magn, cells_y - 1)
        pack_y[half, 0] = field[0, :, pl.ds(row, 1), :]
        pack_y[half, 1] = field[2, :, pl.ds(row, 1), :]

        @pl.when(to_y)
        def _():
            over_y.start()

    def receive(half):
        (to_x, from_x, over_x), (to_y, from_y, over_y) = copies(half)
        elec_new = elec[half // 2 + 1]

        @pl.when(from_y)
        def _():
            over_y.wait_recv()
            if half % 2 == 0:
                row = pl.ds(cells_y - 1, 1)
                magn[0, :, row, :] = magn[0, :, row, :] - COURANT * halo_y[half, 1]
                magn[2, :, row, :] = magn[2, :, row, :] + COURANT * halo_y[half, 0]
            else:
                row = pl.ds(0, 1)
                factor = scale[:, row, :]
                elec_new[0, :, row, :] = elec_new[0, :, row, :] - factor * halo_y[half, 1]
                elec_new[2, :, row, :] = elec_new[2, :, row, :] + factor * halo_y[half, 0]

        @pl.when(from_x)
        def _():
            over_x.wait_recv()
            if half % 2 == 0:
                last = cells_x - 1
                magn[1, last] = magn[1, last] + COURANT * halo_x[half, 1]
                magn[2, last] = magn[2, last] - COURANT * halo_x[half, 0]
            else:
                factor = scale[0]
                elec_new[1, 0] = elec_new[1, 0] + factor * halo_x[half, 1]
                elec_new[2, 0] = elec_new[2, 0] - factor * halo_x[half, 0]

        @pl.when(to_x)
        def _():
            over_x.wait_send()

        @pl.when(to_y)
        def _():
            over_y.wait_send()

    def make_scale():
        def plane(x):
            kind = mat[x]
            eps = jnp.full(kind.shape, eps_ref[0], F32)
            for index in range(1, eps_ref.shape[0]):
                eps = jnp.where(kind == index, eps_ref[index], eps)
            scale[x] = COURANT / eps

        loop(0, cells_x, plane)

    def make_coefs():
        width = 2 * waves * cells_y
        column = iota((8, width), 1)
        wave = column // (2 * cells_y)
        phase = jnp.full((8, width), phase_ref[0], F32)
        for index in range(1, waves):
            phase = jnp.where(wave == index, phase_ref[index], phase)
        angle = phase * (iota((8, width), 0) + 1).astype(F32)
        imaginary = lax.rem(column // cells_y, 2) == 1
        values = jnp.where(imaginary, -jnp.sin(angle), jnp.cos(angle)) / float(waves * STEPS)
        own = iota((cells_y, width), 0) == lax.rem(iota((cells_y, width), 1), cells_y)
        table = jnp.concatenate(
            [jnp.where(own, values[step : step + 1], 0.0) for step in range(STEPS)], axis=0
        )
        coefs[...] = jnp.concatenate(split2(table), axis=0)

    def make_weights(low, high):
        half = STEPS * cells_y

        def plane(index):
            comp, x = lax.rem(index, 3), index // 3
            block = dft[:, :, comp, x].reshape(2 * waves * cells_y, depth)
            both = dot(coefs[...], block)
            weights[:, comp, x] = (both[:half] + both[half:]).reshape(STEPS, cells_y, depth)

        def several(index):
            for extra in range(UNROLL):
                plane(index * UNROLL + extra)

        loop(low, high, several)

    def add_sens(low, high):
        def plane(x):
            total = None
            for step in range(low, high):
                for comp in range(3):
                    term = elec[step + 1][comp, x] * weights[step, comp, x]
                    total = term if total is None else total + term
            for block in range(depth // 128):
                lanes = total[:, block * 128 : (block + 1) * 128]
                sens[block, x] = lanes if low == 0 else sens[block, x] + lanes

        loop(0, cells_x, plane)

    def as_column(values):
        pick = (iota((tiles, tile_x), 0) // tile_y == iota((tiles, tile_x), 1)).astype(BF16)
        spread = dot(pick, values.astype(F32).astype(BF16))
        keep = iota((tiles, tile_y), 1) == lax.rem(iota((tiles, tile_y), 0), tile_y)
        return jnp.sum(jnp.where(keep, spread, 0.0), axis=1, keepdims=True)

    def positions():
        own_row = as_row(owner[...])
        own_column = as_column(owner[...])
        earlier = (own_column == own_row) & (iota((tiles, tiles), 0) < iota((tiles, tiles), 1))
        rank = jnp.sum(jnp.where(earlier, 1.0, 0.0), axis=0, keepdims=True)
        return own_row, own_column, rank

    def send_slots():
        own_row, _, rank = positions()
        mine = (iota((count, tiles), 0).astype(F32) == own_row).astype(BF16)
        place = (iota((128, tiles), 0).astype(F32) == rank).astype(F32)
        labels = (place * (as_row(slot[...]) + 1.0)).astype(BF16)
        table = (
            lax.dot_general(mine, labels, (((1,), (1,)), ((), ())), preferred_element_type=F32)
            - 1.0
        )
        put_slot[...] = table.reshape(count, 1, 128)
        got_slot[me] = put_slot[me]

        def push(step, carry):
            peer = lax.rem(me + step, count)
            pltpu.make_async_remote_copy(
                src_ref=put_slot.at[peer],
                dst_ref=got_slot.at[me],
                send_sem=a2a_sem.at[0],
                recv_sem=a2a_sem.at[1],
                device_id=(peer // size_y, lax.rem(peer, size_y)),
                device_id_type=MESH,
            ).start()
            return carry

        lax.fori_loop(1, count, push, 0)

    def wait_all(buffer, place):
        part = buffer.at[pl.ds(0, count - 1)]
        pltpu.make_async_copy(part, part, a2a_sem.at[place]).wait()

    def make_kernels():
        for index in range(kernels):
            high, low = split2(kern[index])
            kern_high[:, index * voxels : (index + 1) * voxels] = high
            kern_low[:, index * voxels : (index + 1) * voxels] = low

    units = 3 * cells_x // UNROLL

    def share(part):
        make_weights(units * part // 5, units * (part + 1) // 5)

    loads[0].wait()
    pl.semaphore_wait(barrier, count - 1)
    send(0)
    loads[1].wait()
    h_interior(0)
    loads[2].wait()
    make_scale()
    make_coefs()
    receive(0)
    send(1)
    e_interior(0)
    loads[7].wait()
    share(0)
    receive(1)
    send(2)
    h_interior(1)
    for place in (3, 4, 5):
        loads[place].wait()
    send_slots()
    receive(2)
    send(3)
    e_interior(1)
    share(1)
    receive(3)
    send(4)
    h_interior(2)
    share(2)
    receive(4)
    send(5)
    e_interior(2)
    share(3)
    receive(5)
    send(6)
    h_interior(3)
    share(4)
    receive(6)
    send(7)
    e_interior(3)
    loads[6].wait()
    make_kernels()
    add_sens(0, STEPS - 1)
    wait_all(put_slot, 0)
    wait_all(got_slot, 1)
    receive(7)
    add_sens(STEPS - 1, STEPS)

    total = jnp.zeros((tiles, kernels * voxels), F32)
    for a in range(2):
        for b in range(2):
            part = [
                sens[block, pl.ds(a, cells_x // 2, 2), pl.ds(b, cells_y // 2, 2), :]
                for block in range(depth // 128)
            ]
            part = jnp.concatenate([lanes.reshape(tiles, 128) for lanes in part], axis=1)
            high, low = split2(part)
            rows = slice((2 * a + b) * depth, (2 * a + b + 1) * depth)
            big, small = kern_high[rows, :], kern_low[rows, :]
            total = total + dot(high, big) + (dot(low, big) + dot(high, small))
    kinds = as_column(kid[...])
    restricted = jnp.zeros((tiles, voxels), F32)
    for index in range(kernels):
        restricted = restricted + jnp.where(
            kinds == float(index), total[:, index * voxels : (index + 1) * voxels], 0.0
        )

    own_row, _, rank = positions()
    position = own_row * float(capacity) + rank
    placement = (iota((count * capacity, tiles), 0).astype(F32) == position).astype(BF16)
    high, low = split2(restricted)
    put[...] = (dot(placement, high) + dot(placement, low)).reshape(count, capacity, voxels)
    got[me] = put[me]

    def push(step, carry):
        peer = lax.rem(me + step, count)
        pltpu.make_async_remote_copy(
            src_ref=put.at[peer],
            dst_ref=got.at[me],
            send_sem=a2a_sem.at[2],
            recv_sem=a2a_sem.at[3],
            device_id=(peer // size_y, lax.rem(peer, size_y)),
            device_id_type=MESH,
        ).start()
        return carry

    lax.fori_loop(1, count, push, 0)
    wait_all(got, 3)
    wait_all(put, 2)


def finish(capacity, elec, magn, got, got_slot, e_out, h_out, grad_ref, sems):
    stores = [
        pltpu.make_async_copy(elec, e_out, sems.at[0]),
        pltpu.make_async_copy(magn, h_out, sems.at[1]),
    ]
    for store in stores:
        store.start()
    count, _, voxels = got.shape
    received = got_slot[...].reshape(count, 128)[:, :capacity]
    gather = (
        iota((SLOTS, count * capacity), 0).astype(F32) == as_row(received)
    ).astype(BF16)
    high, low = split2(got[...].reshape(count * capacity, voxels))
    grad_ref[...] = dot(gather, high) + dot(gather, low)
    for store in stores:
        store.wait()


def per_device(
    size_x,
    size_y,
    e_field,
    h_field,
    material,
    eps_table,
    forward_dft,
    phase_step,
    interp_kernels,
    kernel_id,
    owner_map,
    slot_map,
):
    count = size_x * size_y
    cells_x, cells_y, depth = material.shape
    kernels, tile_cells, voxels = interp_kernels.shape
    tiles = cells_x * cells_y // 4
    capacity = max(2, (2 * tiles + count - 1) // count)
    field = jax.ShapeDtypeStruct(e_field.shape, F32)
    anywhere = pl.BlockSpec(memory_space=pltpu.HBM)
    halves = 2 * STEPS
    here = pl.BlockSpec(memory_space=pltpu.VMEM)
    state = pl.pallas_call(
        functools.partial(kernel, size_x, size_y, capacity),
        out_shape=(
            pltpu.VMEM(e_field.shape, F32),
            pltpu.VMEM(h_field.shape, F32),
            pltpu.VMEM((count, capacity, voxels), F32),
            pltpu.VMEM((count, 1, 128), F32),
        ),
        in_specs=[pl.BlockSpec(memory_space=pltpu.SMEM)] * 2 + [anywhere] * 8,
        out_specs=(here,) * 4,
        scratch_shapes=[
            pltpu.VMEM((STEPS,) + e_field.shape, F32),
            pltpu.VMEM(material.shape, jnp.int32),
            pltpu.VMEM(material.shape, F32),
            pltpu.VMEM(forward_dft.shape, BF16),
            pltpu.VMEM(interp_kernels.shape, F32),
            pltpu.VMEM((tile_cells, kernels * voxels), BF16),
            pltpu.VMEM((tile_cells, kernels * voxels), BF16),
            pltpu.VMEM(kernel_id.shape, jnp.int32),
            pltpu.VMEM(owner_map.shape, jnp.int32),
            pltpu.VMEM(slot_map.shape, jnp.int32),
            pltpu.VMEM((2 * STEPS * cells_y, 2 * forward_dft.shape[0] * cells_y), BF16),
            pltpu.VMEM((STEPS,) + e_field.shape, F32),
            pltpu.VMEM((depth // 128, cells_x, cells_y, 128), F32),
            pltpu.VMEM((halves, 2, cells_y, depth), F32),
            pltpu.VMEM((halves, 2, cells_x, 1, depth), F32),
            pltpu.VMEM((halves, 2, cells_x, 1, depth), F32),
            pltpu.VMEM((count, capacity, voxels), F32),
            pltpu.VMEM((count, 1, 128), F32),
            pltpu.SemaphoreType.DMA((8,)),
            pltpu.SemaphoreType.DMA((halves,)),
            pltpu.SemaphoreType.DMA((halves,)),
            pltpu.SemaphoreType.DMA((halves,)),
            pltpu.SemaphoreType.DMA((halves,)),
            pltpu.SemaphoreType.DMA((4,)),
        ],
        compiler_params=pltpu.CompilerParams(
            collective_id=0, has_side_effects=True, vmem_limit_bytes=60 * 2**20
        ),
    )(
        eps_table,
        phase_step,
        e_field,
        h_field,
        material,
        forward_dft,
        interp_kernels,
        kernel_id,
        owner_map,
        slot_map,
    )
    return pl.pallas_call(
        functools.partial(finish, capacity),
        out_shape=(field, field, jax.ShapeDtypeStruct((SLOTS, voxels), F32)),
        in_specs=[here] * 4,
        out_specs=(anywhere, anywhere, here),
        scratch_shapes=[pltpu.SemaphoreType.DMA((2,))],
        compiler_params=pltpu.CompilerParams(
            has_side_effects=True, vmem_limit_bytes=8 * 2**20
        ),
    )(*[pltpu.with_memory_space_constraint(part, pltpu.VMEM) for part in state])


def solution(mesh):
    return jax.shard_map(
        functools.partial(per_device, mesh.shape["gx"], mesh.shape["gy"]),
        mesh=mesh,
        in_specs=(
            P(None, "gx", "gy", None),
            P(None, "gx", "gy", None),
            P("gx", "gy", None),
            P(),
            P(None, None, None, "gx", "gy", None),
            P(),
            P(),
            P("gx", "gy"),
            P("gx", "gy"),
            P("gx", "gy"),
        ),
        out_specs=(P(None, "gx", "gy", None), P(None, "gx", "gy", None), P(("gx", "gy"), None)),
        check_vma=False,
    )
```
